32 devices in a mesh: groups: 1, tensor: 16 (over z, y, x), sub: 2 (over core).
Axes of the slice: x: 2, y: 2, z: 4, core: 2. Of those that a mesh axis runs over, the one named last changes fastest.
Arguments:
- stored: bfloat16 [8192, 32768], P(('tensor', 'sub')), may hold values from -0.0625 to 0.0625
- tokens: bfloat16 [256, 8192], P(('groups', 'tensor')), may hold values from -6 to 6
- owner_map: int32 [256], replicated, may hold values from 0 to 255, each once
- live_count: int32 [1], P('groups'), may hold values from 128 to 256
Outputs:
- serving_out: bfloat16 [256, 32768], P('groups', ('tensor', 'sub'))
The draws below stay inside these ranges and needn't reach their ends.
Inputs may be any that keep to these rules, and one draw needn't show every extreme that they name: `owner_map`: each of the 256 saved column blocks is named exactly once. Rows from live_count on are padding.
All inputs are finite; a program needn't handle non-finite values.
Results may differ from the reference program's by a relative error of at most 0.001.
Values may be sent and summed in bfloat16 or wider, within the bound.
A program may use at most 128 MiB of HBM per device.

```python
import jax
import jax.numpy as jnp

D = 8192
FF = 32768
BLOCK = 128
TOKENS = 256
NB = 256


def block_levels(rng, extent, cuts, least, top_value):
    factor_of = 1.0
    for axis_at, shards_of in cuts:
        heights = jax.random.uniform(jax.random.fold_in(jax.random.fold_in(rng, 6), axis_at), (shards_of,), jnp.float32, least / len(cuts), top_value / len(cuts))
        factor_of = factor_of * jnp.repeat(jnp.exp(heights), extent[axis_at] // shards_of).reshape((-1,) + (1,) * (len(extent) - 1 - axis_at))
    return factor_of


def noise(key, dims, width, most, cuts=(), kind=jnp.bfloat16):
    factor_of = block_levels(key, dims, cuts, -0.22, 0.18) if cuts else 1.0
    array = jax.random.normal(key, dims, jnp.float32) * width * factor_of
    return jnp.minimum(jnp.maximum(array, -most), most).astype(kind)


def setup_inputs(seed: int = 0, part: int = 0) -> dict:
    seeds = jax.random.split(jax.random.key(seed), 5)
    part_keys = jax.random.split(jax.random.fold_in(seeds[4], part), 5)
    stored = noise(seeds[0], (D, FF), D ** -0.5, 0.0625, ((0, 32),))
    tokens = noise(part_keys[1], (TOKENS, D), 1.0, 6.0, ((0, 16),))
    owner_map = jax.random.permutation(seeds[2], NB).astype(jnp.int32)
    live_count = jax.random.randint(part_keys[3], (1,), TOKENS // 2, TOKENS + 1).astype(jnp.int32)
    return {"stored": stored, "tokens": tokens, "owner_map": owner_map, "live_count": live_count}


def reference(stored, tokens, owner_map, live_count):
    product = jnp.dot(tokens, stored, preferred_element_type=jnp.float32)
    regrouped = jnp.take(product.reshape(TOKENS, NB, BLOCK), owner_map, axis=1).reshape(TOKENS, FF)
    row_ids = jnp.arange(TOKENS, dtype=jnp.int32)
    keep = (row_ids < live_count[0])[:, None]
    return jnp.where(keep, regrouped, jnp.float32(0.0)).astype(jnp.bfloat16)
```

```python
import functools

import jax
import jax.numpy as jnp
from jax import lax
from jax.experimental import pallas as pl
from jax.experimental.pallas import tpu as pltpu
from jax.sharding import PartitionSpec as P

MESH = pl.DeviceIdType.MESH
VMEM_LIMIT = 67043328


def portable(stored, tokens, owner_map, live_count):
    row_count = stored.shape[0]
    block_count = owner_map.shape[0]
    width = stored.shape[1] // block_count
    devices = lax.axis_size(("tensor", "sub"))
    per_dev = block_count // devices
    ordered = jnp.take(stored.reshape(row_count, block_count, width), owner_map, axis=1)
    gathered = lax.all_gather(tokens, "tensor", axis=0, tiled=True)
    sectioned = ordered.reshape(row_count, devices, per_dev, width)
    piece = lax.all_to_all(sectioned, ("tensor", "sub"), split_axis=1, concat_axis=0, tiled=True)
    weights = piece.reshape(piece.shape[0], piece.shape[2], piece.shape[3])
    result = jnp.einsum("td,dkc->tkc", gathered, weights, preferred_element_type=jnp.float32)
    product = result.reshape(result.shape[0], per_dev * width)
    row_ids = lax.broadcasted_iota(jnp.int32, (product.shape[0], 1), 0)
    keep = row_ids < live_count[0]
    return jnp.where(keep, product, jnp.float32(0.0)).astype(jnp.bfloat16)


def kernel(T, Z, own_rows, block, half, map_ref, tok_ref, w_hbm, out_ref,
           w, tok, stage, wr, p, r1, r2, rz,
           w_sem, ts, tr, ss, sr, s1s, s1r, s2s, s2r, zs, zr):
    t = lax.axis_index("tensor")
    s = lax.axis_index("sub")
    x, y, z = lax.rem(t, 2), lax.rem(t // 2, 2), t // 4
    depth = w.shape[1]
    other = 1 - s
    x_far = t + 1 - 2 * x
    y_far = t + 2 - 4 * y
    firsts = 4 * Z

    def load_block(b, carry):
        at = pl.multiple_of(b * block, block)
        pltpu.make_async_copy(w_hbm.at[:, pl.ds(at, block)], w.at[b], w_sem).start()
        return carry

    lax.fori_loop(0, w.shape[0], load_block, 0)

    barrier = pltpu.get_barrier_semaphore()
    for r in range(1, T):
        pl.semaphore_signal(barrier, inc=1, device_id={"tensor": lax.rem(t + r, T), "sub": s}, device_id_type=MESH)
    pl.semaphore_signal(barrier, inc=1, device_id={"tensor": t, "sub": other}, device_id_type=MESH)
    pl.semaphore_wait(barrier, T)

    def token_copy(r):
        to = lax.rem(t + r, T)
        return pltpu.make_async_remote_copy(
            src_ref=tok_ref.at[:, pl.ds(pl.multiple_of(to * 2 * depth, 2 * depth), 2 * depth)],
            dst_ref=tok.at[pl.ds(pl.multiple_of(t * own_rows, own_rows), own_rows), :],
            send_sem=ts.at[r], recv_sem=tr.at[r],
            device_id={"tensor": to, "sub": s}, device_id_type=MESH)

    for r in range(1, T):
        token_copy(r).start()
    tok[pl.ds(pl.multiple_of(t * own_rows, own_rows), own_rows), :] = (
        tok_ref[:, pl.ds(pl.multiple_of(t * 2 * depth, 2 * depth), 2 * depth)])

    def sub_copy(h, j):
        return pltpu.make_async_remote_copy(
            src_ref=stage.at[j], dst_ref=wr.at[4 * h + j],
            send_sem=ss.at[j], recv_sem=sr.at[4 * h + j],
            device_id={"tensor": t, "sub": other}, device_id_type=MESH)

    def first_copy(g, j):
        return pltpu.make_async_remote_copy(
            src_ref=p.at[4 * g + j], dst_ref=r1.at[4 * g + j],
            send_sem=s1s.at[4 * g + j], recv_sem=s1r.at[4 * g + j],
            device_id={"tensor": y_far if j % 2 else x_far, "sub": s}, device_id_type=MESH)

    def second_copy(g, j):
        return pltpu.make_async_remote_copy(
            src_ref=p.at[firsts + 4 * g + j], dst_ref=r2.at[2 * g + j],
            send_sem=s2s.at[2 * g + j], recv_sem=s2r.at[2 * g + j],
            device_id={"tensor": x_far if j % 2 else y_far, "sub": s}, device_id_type=MESH)

    def z_copy(g, j):
        to = lax.rem(t + 4 * (g + 1), T)
        return pltpu.make_async_remote_copy(
            src_ref=p.at[firsts + 4 * g + 2 + j], dst_ref=rz.at[2 * g + j],
            send_sem=zs.at[2 * g + j], recv_sem=zr.at[2 * g + j],
            device_id={"tensor": to, "sub": s}, device_id_type=MESH)

    def first_block(h, j, sub):
        kept, g = h // Z, lax.rem(h, Z)
        rx = (1 - kept, 1, 1 - kept, 0)[j]
        ry = (1, 1 - kept, 0, 1 - kept)[j]
        to = lax.rem(z + g + 1, Z) * 4 + lax.rem(y + ry, 2) * 2 + lax.rem(x + rx, 2)
        return (2 * to + sub) * (2 * half) + (j % 2) * half

    def columns(base, m):
        return w[map_ref[base + m]]

    def fill(h, j):
        base = first_block(h, j, other)
        for m in range(half):
            stage[j, :, m * block:(m + 1) * block] = columns(base, m)
        sub_copy(h, j).start()

    pltpu.make_async_copy(w, w, w_sem).wait()
    for j in range(4):
        fill(0, j)
    for r in range(1, T):
        token_copy(r).wait()

    rows = p.shape[1]

    def body(h, carry):
        mine = tok[0:rows, pl.ds(pl.multiple_of(s * depth, depth), depth)]
        theirs = tok[0:rows, pl.ds(pl.multiple_of(other * depth, depth), depth)]
        for j in range(4):
            base = first_block(h, j, s)
            own = jnp.concatenate([columns(base, m) for m in range(half)], axis=1)
            total = jnp.dot(mine, own, preferred_element_type=jnp.float32)
            sub_copy(h, j).wait()
            total += jnp.dot(theirs, wr[4 * h + j], preferred_element_type=jnp.float32)
            p[4 * h + j] = total

            @pl.when(h < 2)
            def _():
                first_copy(h, j).start()

            @pl.when(h < 2 * Z - 1)
            def _():
                fill(h + 1, j)
        return carry

    lax.fori_loop(0, 2 * Z, body, 0)

    def second(g):
        for j in range(2):
            second_copy(g, j).wait_recv()
            p[firsts + 4 * g + 2 + j] += r2[2 * g + j]
            if g < Z - 1:
                z_copy(g, j).start()

    for g in range(Z):
        for j in range(2):
            first_copy(g, j).wait_recv()
            p[firsts + 4 * g + j] += r1[4 * g + j]
            second_copy(g, j).start()
        if g + 2 < Z:
            for j in range(4):
                first_copy(g + 2, j).start()
        for j in range(2, 4):
            first_copy(g, j).wait_recv()
            p[firsts + 4 * g + j] += r1[4 * g + j]
        if g >= 1:
            second(g - 1)
    second(Z - 1)
    wide = half * block
    for j in range(2):
        total = p[firsts + 4 * (Z - 1) + 2 + j]
        for g in range(Z - 1):
            z_copy(g, j).wait_recv()
            total += rz[2 * g + j]
        out_ref[0:rows, j * wide:(j + 1) * wide] = total.astype(out_ref.dtype)
    for g in range(Z):
        for j in range(4):
            first_copy(g, j).wait_send()
        for j in range(2):
            second_copy(g, j).wait_send()
            if g < Z - 1:
                z_copy(g, j).wait_send()


def plan(depth, ff, own_rows, block, T, n_blocks):
    Z = T // 4
    wide = ff // (4 * T)
    rows = own_rows * T
    sems = pltpu.SemaphoreType.DMA
    f32, bf16 = jnp.float32, jnp.bfloat16
    return [
        pltpu.VMEM((n_blocks, depth, block), bf16),
        pltpu.VMEM((rows, 2 * depth), bf16),
        pltpu.VMEM((4, depth, wide), bf16),
        pltpu.VMEM((8 * Z, depth, wide), bf16),
        pltpu.VMEM((8 * Z, rows, wide), f32),
        pltpu.VMEM((4 * Z, rows, wide), f32),
        pltpu.VMEM((2 * Z, rows, wide), f32),
        pltpu.VMEM((2 * Z, rows, wide), f32),
    ] + [sems(()), sems((T,)), sems((T,)), sems((4,)), sems((8 * Z,)), sems((4 * Z,)), sems((4 * Z,)),
         sems((2 * Z,)), sems((2 * Z,)), sems((2 * Z,)), sems((2 * Z,))]


def fits(depth, ff, own_rows, block, T, subs, n_blocks):
    if T % 4 or T < 8 or subs != 2 or n_blocks % (4 * T):
        return False
    rows, wide, Z = own_rows * T, ff // (4 * T), T // 4
    used = 2 * (depth * ff + rows * 2 * depth + (4 + 8 * Z) * depth * wide) + 4 * (16 * Z * rows * wide)
    return used + (4 << 20) < VMEM_LIMIT


def on_device(stored, tokens, owner_map, live_count):
    depth, ff = stored.shape
    own_rows = tokens.shape[0]
    n_blocks = owner_map.shape[0]
    block = ff // n_blocks
    T, subs = lax.axis_size("tensor"), lax.axis_size("sub")
    if not fits(depth, ff, own_rows, block, T, subs, n_blocks):
        return portable(stored, tokens, owner_map, live_count)
    rows = own_rows * T
    half = n_blocks // (4 * T)
    product = pl.pallas_call(
        functools.partial(kernel, T, T // 4, own_rows, block, half),
        out_shape=jax.ShapeDtypeStruct((rows, ff // (2 * T)), jnp.bfloat16),
        in_specs=[pl.BlockSpec(memory_space=pltpu.SMEM), pl.BlockSpec(memory_space=pltpu.VMEM),
                  pl.BlockSpec(memory_space=pl.ANY)],
        out_specs=pl.BlockSpec(memory_space=pltpu.VMEM),
        scratch_shapes=plan(depth, ff, own_rows, block, T, n_blocks),
        compiler_params=pltpu.CompilerParams(
            collective_id=0, has_side_effects=True, vmem_limit_bytes=VMEM_LIMIT),
    )(owner_map, tokens, stored)
    keep = lax.broadcasted_iota(jnp.int32, (rows, 1), 0) < live_count[0]
    return jnp.where(keep, product, jnp.bfloat16(0.0))


def solution(mesh):
    placed = (P(("tensor", "sub"), None), P(("groups", "tensor"), None), P(), P("groups"))
    return jax.shard_map(
        on_device,
        mesh=mesh,
        in_specs=placed,
        out_specs=P("groups", ("tensor", "sub")),
        check_vma=False,
    )
```

```python
import functools

import jax
import jax.numpy as jnp
from jax import lax
from jax.experimental import pallas as pl
from jax.experimental.pallas import tpu as pltpu
from jax.sharding import PartitionSpec as P

MESH = pl.DeviceIdType.MESH
VMEM_LIMIT = 67043328


def portable(stored, tokens, owner_map, live_count):
    row_count = stored.shape[0]
    block_count = owner_map.shape[0]
    width = stored.shape[1] // block_count
    devices = lax.axis_size(("tensor", "sub"))
    per_dev = block_count // devices
    ordered = jnp.take(stored.reshape(row_count, block_count, width), owner_map, axis=1)
    gathered = lax.all_gather(tokens, "tensor", axis=0, tiled=True)
    sectioned = ordered.reshape(row_count, devices, per_dev, width)
    piece = lax.all_to_all(sectioned, ("tensor", "sub"), split_axis=1, concat_axis=0, tiled=True)
    weights = piece.reshape(piece.shape[0], piece.shape[2], piece.shape[3])
    result = jnp.einsum("td,dkc->tkc", gathered, weights, preferred_element_type=jnp.float32)
    product = result.reshape(result.shape[0], per_dev * width)
    row_ids = lax.broadcasted_iota(jnp.int32, (product.shape[0], 1), 0)
    keep = row_ids < live_count[0]
    return jnp.where(keep, product, jnp.float32(0.0)).astype(jnp.bfloat16)


def kernel(T, Z, own_rows, block, half, map_ref, tok_ref, w_hbm, out_ref,
           w, tok, stage, wr, p, r1, r2, rz,
           w_sem, ts, tr, ss, sr, s1s, s1r, s2s, s2r, zs, zr):
    t = lax.axis_index("tensor")
    s = lax.axis_index("sub")
    x, y, z = lax.rem(t, 2), lax.rem(t // 2, 2), t // 4
    depth = w.shape[1]
    other = 1 - s
    x_far = t + 1 - 2 * x
    y_far = t + 2 - 4 * y
    firsts = 4 * Z
    rows = p.shape[1]
    order = sorted(range(1, Z), key=lambda k: -min(k, Z - k)) + [0]

    def z_offset(g):
        return sum(jnp.where(g == i, k, 0) for i, k in enumerate(order) if k)

    def load_block(b, carry):
        at = pl.multiple_of(b * block, block)
        pltpu.make_async_copy(w_hbm.at[:, pl.ds(at, block)], w.at[b], w_sem).start()
        return carry

    lax.fori_loop(0, w.shape[0], load_block, 0)

    barrier = pltpu.get_barrier_semaphore()
    for r in range(1, T):
        pl.semaphore_signal(barrier, inc=1, device_id={"tensor": lax.rem(t + r, T), "sub": s}, device_id_type=MESH)
    pl.semaphore_signal(barrier, inc=1, device_id={"tensor": t, "sub": other}, device_id_type=MESH)
    pl.semaphore_wait(barrier, T)

    def token_copy(r):
        to = lax.rem(t + r, T)
        return pltpu.make_async_remote_copy(
            src_ref=tok_ref.at[:, pl.ds(pl.multiple_of(to * 2 * depth, 2 * depth), 2 * depth)],
            dst_ref=tok.at[pl.ds(pl.multiple_of(t * own_rows, own_rows), own_rows), :],
            send_sem=ts.at[r], recv_sem=tr.at[r],
            device_id={"tensor": to, "sub": s}, device_id_type=MESH)

    for r in range(1, T):
        token_copy(r).start()
    tok[pl.ds(pl.multiple_of(t * own_rows, own_rows), own_rows), :] = (
        tok_ref[:, pl.ds(pl.multiple_of(t * 2 * depth, 2 * depth), 2 * depth)])

    def sub_copy(h, j):
        return pltpu.make_async_remote_copy(
            src_ref=stage.at[j], dst_ref=wr.at[4 * h + j],
            send_sem=ss.at[j], recv_sem=sr.at[4 * h + j],
            device_id={"tensor": t, "sub": other}, device_id_type=MESH)

    def first_copy(g, j):
        return pltpu.make_async_remote_copy(
            src_ref=p.at[4 * g + j], dst_ref=r1.at[4 * g + j],
            send_sem=s1s.at[4 * g + j], recv_sem=s1r.at[4 * g + j],
            device_id={"tensor": y_far if j % 2 else x_far, "sub": s}, device_id_type=MESH)

    def second_copy(g, j):
        return pltpu.make_async_remote_copy(
            src_ref=p.at[firsts + 4 * g + j], dst_ref=r2.at[2 * g + j],
            send_sem=s2s.at[2 * g + j], recv_sem=s2r.at[2 * g + j],
            device_id={"tensor": x_far if j % 2 else y_far, "sub": s}, device_id_type=MESH)

    def z_copy(g, j):
        to = lax.rem(t + 4 * z_offset(g), T)
        return pltpu.make_async_remote_copy(
            src_ref=p.at[firsts + 4 * g + 2 + j], dst_ref=rz.at[2 * g + j],
            send_sem=zs.at[2 * g + j], recv_sem=zr.at[2 * g + j],
            device_id={"tensor": to, "sub": s}, device_id_type=MESH)

    def first_block(h, j, sub):
        kept, g = lax.rem(h, 2), h // 2
        rx = (1 - kept, 1, 1 - kept, 0)[j]
        ry = (1, 1 - kept, 0, 1 - kept)[j]
        to = lax.rem(z + z_offset(g), Z) * 4 + lax.rem(y + ry, 2) * 2 + lax.rem(x + rx, 2)
        return (2 * to + sub) * (2 * half) + (j % 2) * half

    def columns(base, m):
        return w[map_ref[base + m]]

    def fill(h, j):
        base = first_block(h, j, other)
        for m in range(half):
            stage[j, :, m * block:(m + 1) * block] = columns(base, m)
        sub_copy(h, j).start()

    pltpu.make_async_copy(w, w, w_sem).wait()
    for j in range(4):
        fill(0, j)
    for r in range(1, T):
        token_copy(r).wait()

    def compute(q, carry):
        kept, g = lax.rem(q, 2), q // 2
        mine = tok[0:rows, pl.ds(pl.multiple_of(s * depth, depth), depth)]
        theirs = tok[0:rows, pl.ds(pl.multiple_of(other * depth, depth), depth)]
        for j in range(4):
            base = first_block(q, j, s)
            own = jnp.concatenate([columns(base, m) for m in range(half)], axis=1)
            total = jnp.dot(mine, own, preferred_element_type=jnp.float32)
            sub_copy(q, j).wait()
            total += jnp.dot(theirs, wr[4 * q + j], preferred_element_type=jnp.float32)
            p[firsts * kept + 4 * g + j] = total

            @pl.when(q == 0)
            def _():
                first_copy(0, j).start()

            @pl.when(q < 2 * Z - 1)
            def _():
                fill(q + 1, j)
        return carry

    def second(g):
        for j in range(2):
            second_copy(g, j).wait_recv()
            p[firsts + 4 * g + 2 + j] += r2[2 * g + j]

    def step(at, carry):
        g = at - 2

        @pl.when(g >= 0)
        def _():
            for j in range(2):
                first_copy(g, j).wait_recv()
                p[firsts + 4 * g + j] += r1[4 * g + j]
                second_copy(g, j).start()

            @pl.when(g < Z - 1)
            def _():
                for j in range(4):
                    first_copy(g + 1, j).start()

            for j in range(2, 4):
                first_copy(g, j).wait_recv()
                p[firsts + 4 * g + j] += r1[4 * g + j]

        lax.fori_loop(jnp.maximum(2 * g + 3, 0), jnp.minimum(2 * g + 5, 2 * Z), compute, 0)

        @pl.when(g >= 1)
        def _():
            second(g - 1)
            for j in range(2):
                z_copy(g - 1, j).start()
        return carry

    lax.fori_loop(0, Z + 2, step, 0)
    second(Z - 1)
    wide = half * block
    for j in range(2):
        total = p[firsts + 4 * (Z - 1) + 2 + j]
        for g in range(Z - 1):
            z_copy(g, j).wait_recv()
            total += rz[2 * g + j]
        out_ref[0:rows, j * wide:(j + 1) * wide] = total.astype(out_ref.dtype)
    for g in range(Z):
        for j in range(4):
            first_copy(g, j).wait_send()
        for j in range(2):
            second_copy(g, j).wait_send()
            if g < Z - 1:
                z_copy(g, j).wait_send()


def plan(depth, ff, own_rows, block, T, n_blocks, live):
    Z = T // 4
    wide = ff // (4 * T)
    rows = own_rows * T
    sems = pltpu.SemaphoreType.DMA
    f32, bf16 = jnp.float32, jnp.bfloat16
    return [
        pltpu.VMEM((n_blocks, depth, block), bf16),
        pltpu.VMEM((rows, 2 * depth), bf16),
        pltpu.VMEM((4, depth, wide), bf16),
        pltpu.VMEM((8 * Z, depth, wide), bf16),
        pltpu.VMEM((8 * Z, live, wide), f32),
        pltpu.VMEM((4 * Z, live, wide), f32),
        pltpu.VMEM((2 * Z, live, wide), f32),
        pltpu.VMEM((2 * Z, live, wide), f32),
    ] + [sems(()), sems((T,)), sems((T,)), sems((4,)), sems((8 * Z,)), sems((4 * Z,)), sems((4 * Z,)),
         sems((2 * Z,)), sems((2 * Z,)), sems((2 * Z,)), sems((2 * Z,))]


def fits(depth, ff, own_rows, block, T, subs, n_blocks):
    if T % 4 or T < 8 or subs != 2 or n_blocks % (4 * T):
        return False
    rows, wide, Z = own_rows * T, ff // (4 * T), T // 4
    used = 2 * (depth * ff + rows * 2 * depth + (4 + 8 * Z) * depth * wide) + 4 * (16 * Z * rows * wide)
    return used + (4 << 20) < VMEM_LIMIT


def on_device(stored, tokens, owner_map, live_count):
    depth, ff = stored.shape
    own_rows = tokens.shape[0]
    n_blocks = owner_map.shape[0]
    block = ff // n_blocks
    T, subs = lax.axis_size("tensor"), lax.axis_size("sub")
    if not fits(depth, ff, own_rows, block, T, subs, n_blocks):
        return portable(stored, tokens, owner_map, live_count)
    rows = own_rows * T
    half = n_blocks // (4 * T)
    unit = max(rows // 8, 16)
    sizes = [n for n in range(rows - 4 * unit, rows, unit) if n > 0] + [rows]

    def call(n, which):
        return pl.pallas_call(
            functools.partial(kernel, T, T // 4, own_rows, block, half),
            out_shape=jax.ShapeDtypeStruct((rows, ff // (2 * T)), jnp.bfloat16),
            in_specs=[pl.BlockSpec(memory_space=pltpu.SMEM), pl.BlockSpec(memory_space=pltpu.VMEM),
                      pl.BlockSpec(memory_space=pl.ANY)],
            out_specs=pl.BlockSpec(memory_space=pltpu.VMEM),
            scratch_shapes=plan(depth, ff, own_rows, block, T, n_blocks, n),
            compiler_params=pltpu.CompilerParams(
                collective_id=which, has_side_effects=True, vmem_limit_bytes=VMEM_LIMIT),
        )

    most = live_count[0]
    if lax.axis_size("groups") > 1:
        most = lax.pmax(most, "groups")
    which = sum((most > n).astype(jnp.int32) for n in sizes[:-1])
    product = lax.switch(which, [call(n, i) for i, n in enumerate(sizes)], owner_map, tokens, stored)
    keep = lax.broadcasted_iota(jnp.int32, (rows, 1), 0) < live_count[0]
    return jnp.where(keep, product, jnp.bfloat16(0.0))


def solution(mesh):
    placed = (P(("tensor", "sub"), None), P(("groups", "tensor"), None), P(), P("groups"))
    return jax.shard_map(
        on_device,
        mesh=mesh,
        in_specs=placed,
        out_specs=P("groups", ("tensor", "sub")),
        check_vma=False,
    )
```

```python
import functools

import jax
import jax.numpy as jnp
from jax import lax
from jax.experimental import pallas as pl
from jax.experimental.pallas import tpu as pltpu
from jax.sharding import PartitionSpec as P

MESH = pl.DeviceIdType.MESH
VMEM_LIMIT = 67043328


def portable(stored, tokens, owner_map, live_count):
    row_count = stored.shape[0]
    block_count = owner_map.shape[0]
    width = stored.shape[1] // block_count
    devices = lax.axis_size(("tensor", "sub"))
    per_dev = block_count // devices
    ordered = jnp.take(stored.reshape(row_count, block_count, width), owner_map, axis=1)
    gathered = lax.all_gather(tokens, "tensor", axis=0, tiled=True)
    sectioned = ordered.reshape(row_count, devices, per_dev, width)
    piece = lax.all_to_all(sectioned, ("tensor", "sub"), split_axis=1, concat_axis=0, tiled=True)
    weights = piece.reshape(piece.shape[0], piece.shape[2], piece.shape[3])
    result = jnp.einsum("td,dkc->tkc", gathered, weights, preferred_element_type=jnp.float32)
    product = result.reshape(result.shape[0], per_dev * width)
    row_ids = lax.broadcasted_iota(jnp.int32, (product.shape[0], 1), 0)
    keep = row_ids < live_count[0]
    return jnp.where(keep, product, jnp.float32(0.0)).astype(jnp.bfloat16)


def kernel(T, own_rows, block, parts, map_ref, tok_ref, w_hbm, out_ref, w, tok, *refs):
    t = lax.axis_index("tensor")
    s = lax.axis_index("sub")
    depth = w.shape[1]
    other = 1 - s
    n = len(parts)
    bufs = [refs[7 * i:7 * i + 7] for i in range(n)]
    w_sem, ts, tr, ss, sr, cs, cr = refs[7 * n:]
    rows = bufs[0][2].shape[1]
    bits = [lax.rem(t // 2 ** k, 2) for k in range(4)]
    far = [t + 2 ** k * (1 - 2 * bits[k]) for k in range(4)]
    per_dev = sum(count for count, _ in parts)
    starts = [sum(count for count, _ in parts[:i]) for i in range(n)]

    def load_block(b, carry):
        at = pl.multiple_of(b * block, block)
        pltpu.make_async_copy(w_hbm.at[:, pl.ds(at, block)], w.at[b], w_sem).start()
        return carry

    lax.fori_loop(0, w.shape[0], load_block, 0)

    barrier = pltpu.get_barrier_semaphore()
    for r in range(1, T):
        pl.semaphore_signal(barrier, inc=1, device_id={"tensor": lax.rem(t + r, T), "sub": s}, device_id_type=MESH)
    pl.semaphore_signal(barrier, inc=1, device_id={"tensor": t, "sub": other}, device_id_type=MESH)
    pl.semaphore_wait(barrier, T)

    def token_copy(r):
        to = lax.rem(t + r, T)
        return pltpu.make_async_remote_copy(
            src_ref=tok_ref.at[:, pl.ds(pl.multiple_of(to * 2 * depth, 2 * depth), 2 * depth)],
            dst_ref=tok.at[pl.ds(pl.multiple_of(t * own_rows, own_rows), own_rows), :],
            send_sem=ts.at[r], recv_sem=tr.at[r],
            device_id={"tensor": to, "sub": s}, device_id_type=MESH)

    for r in range(1, T):
        token_copy(r).start()
    tok[pl.ds(pl.multiple_of(t * own_rows, own_rows), own_rows), :] = (
        tok_ref[:, pl.ds(pl.multiple_of(t * 2 * depth, 2 * depth), 2 * depth)])

    def sub_copy(q, j, i):
        stage, wr = bufs[i][:2]
        return pltpu.make_async_remote_copy(
            src_ref=stage.at[j], dst_ref=wr.at[2 * q + j],
            send_sem=ss.at[2 * i + j], recv_sem=sr.at[16 * i + 2 * q + j],
            device_id={"tensor": t, "sub": other}, device_id_type=MESH)

    def halving(i, level, slot, at):
        place = 15 * i + (0, 8, 12, 14)[level] + at
        return pltpu.make_async_remote_copy(
            src_ref=bufs[i][2].at[slot], dst_ref=bufs[i][3 + level].at[at],
            send_sem=cs.at[place], recv_sem=cr.at[place],
            device_id={"tensor": far[parts[i][1][level]], "sub": s}, device_id_type=MESH)

    def first(g, j, i):
        return halving(i, 0, 4 * g + j, 2 * g + j)

    def second(g, i):
        return halving(i, 1, 4 * g + 2, g)

    def third(g, i):
        return halving(i, 2, 4 * g + 3, g)

    def fourth(i):
        return halving(i, 3, 11, 0)

    def add(i, level, slot, at):
        bufs[i][2][slot] += bufs[i][3 + level][at]

    def first_block(q, j, i, sub):
        g = q // 2
        flips = (1 - lax.rem(q, 2), 1 - j, 1 - g // 2, 1 - lax.rem(g, 2))
        to = 0
        for k, flip in zip(parts[i][1], flips):
            to += lax.rem(bits[k] + flip, 2) * 2 ** k
        return (2 * to + sub) * per_dev + starts[i]

    def columns(base, m):
        return w[map_ref[base + m]]

    def fill(q, j, i):
        base = first_block(q, j, i, other)
        for m in range(parts[i][0]):
            bufs[i][0][j, :, m * block:(m + 1) * block] = columns(base, m)
        sub_copy(q, j, i).start()

    pltpu.make_async_copy(w, w, w_sem).wait()
    for j in range(2):
        for i in range(n):
            fill(0, j, i)
    for r in range(1, T):
        token_copy(r).wait()

    def compute(q, carry):
        kept, g = lax.rem(q, 2), q // 2
        mine = tok[0:rows, pl.ds(pl.multiple_of(s * depth, depth), depth)]
        theirs = tok[0:rows, pl.ds(pl.multiple_of(other * depth, depth), depth)]
        for j in range(2):
            for i in range(n):
                base = first_block(q, j, i, s)
                own = jnp.concatenate([columns(base, m) for m in range(parts[i][0])], axis=1)
                total = jnp.dot(mine, own, preferred_element_type=jnp.float32)
                sub_copy(q, j, i).wait()
                total += jnp.dot(theirs, bufs[i][1][2 * q + j], preferred_element_type=jnp.float32)
                bufs[i][2][4 * g + 2 * kept + j] = total

                @pl.when(q == 0)
                def _():
                    first(0, j, i).start()

                @pl.when(q < 7)
                def _():
                    fill(q + 1, j, i)
        return carry

    def finish(g):
        for i in range(n):
            second(g, i).wait_recv()
            add(i, 1, 4 * g + 3, g)

    def step(at, carry):
        g = at - 2

        @pl.when(g >= 0)
        def _():
            for i in range(n):
                first(g, 0, i).wait_recv()
                add(i, 0, 4 * g + 2, 2 * g)
                second(g, i).start()

            @pl.when(g < 3)
            def _():
                for j in range(2):
                    for i in range(n):
                        first(g + 1, j, i).start()

            for i in range(n):
                first(g, 1, i).wait_recv()
                add(i, 0, 4 * g + 3, 2 * g + 1)

        lax.fori_loop(jnp.maximum(2 * g + 3, 0), jnp.minimum(2 * g + 5, 8), compute, 0)

        @pl.when(g >= 1)
        def _():
            finish(g - 1)

            @pl.when(g < 3)
            def _():
                for i in range(n):
                    third(g - 1, i).start()

            @pl.when(g == 3)
            def _():
                for i in range(n):
                    third(0, i).wait_recv()
                    add(i, 2, 11, 0)
                    fourth(i).start()
        return carry

    lax.fori_loop(0, 6, step, 0)
    for i in range(n):
        total = bufs[i][2][15]
        third(1, i).wait_recv()
        total += bufs[i][5][1]
        second(3, i).wait_recv()
        total += bufs[i][4][3]
        fourth(i).wait_recv()
        total += bufs[i][6][0]
        out_ref[0:rows, starts[i] * block:(starts[i] + parts[i][0]) * block] = total.astype(out_ref.dtype)
    for i in range(n):
        for g in range(4):
            for j in range(2):
                first(g, j, i).wait_send()
            second(g, i).wait_send()
        for g in range(2):
            third(g, i).wait_send()
        fourth(i).wait_send()


def split(per_dev):
    last = per_dev // 4
    rest = per_dev - last
    return (((rest + 1) // 2, (0, 1, 2, 3)), (rest // 2, (1, 0, 2, 3)), (last, (2, 3, 0, 1)))


def plan(depth, n_blocks, own_rows, block, T, parts, live):
    sems = pltpu.SemaphoreType.DMA
    f32, bf16 = jnp.float32, jnp.bfloat16
    n = len(parts)
    shapes = [pltpu.VMEM((n_blocks, depth, block), bf16), pltpu.VMEM((own_rows * T, 2 * depth), bf16)]
    for count, _ in parts:
        wide = count * block
        shapes += [pltpu.VMEM((2, depth, wide), bf16), pltpu.VMEM((16, depth, wide), bf16)]
        shapes += [pltpu.VMEM((k, live, wide), f32) for k in (16, 8, 4, 2, 1)]
    return shapes + [sems(()), sems((T,)), sems((T,)), sems((2 * n,)), sems((16 * n,)), sems((15 * n,)), sems((15 * n,))]


def fits(depth, ff, own_rows, T, subs, n_blocks):
    if T.bit_length() != 5 or T & (T - 1) or subs != 2 or n_blocks % (8 * T):
        return False
    rows, wide = own_rows * T, ff // (2 * T)
    used = 2 * (depth * ff + rows * 2 * depth + 18 * depth * wide) + 4 * 31 * rows * wide
    return used + (4 << 20) < VMEM_LIMIT


def on_device(stored, tokens, owner_map, live_count):
    depth, ff = stored.shape
    own_rows = tokens.shape[0]
    n_blocks = owner_map.shape[0]
    block = ff // n_blocks
    T, subs = lax.axis_size("tensor"), lax.axis_size("sub")
    if not fits(depth, ff, own_rows, T, subs, n_blocks):
        return portable(stored, tokens, owner_map, live_count)
    rows = own_rows * T
    parts = split(n_blocks // (2 * T))
    unit = max(rows // 8, 16)
    sizes = [n for n in range(rows - 4 * unit, rows, unit) if n > 0] + [rows]

    def call(n, which):
        return pl.pallas_call(
            functools.partial(kernel, T, own_rows, block, parts),
            out_shape=jax.ShapeDtypeStruct((rows, ff // (2 * T)), jnp.bfloat16),
            in_specs=[pl.BlockSpec(memory_space=pltpu.SMEM), pl.BlockSpec(memory_space=pltpu.VMEM),
                      pl.BlockSpec(memory_space=pl.ANY)],
            out_specs=pl.BlockSpec(memory_space=pltpu.VMEM),
            scratch_shapes=plan(depth, n_blocks, own_rows, block, T, parts, n),
            compiler_params=pltpu.CompilerParams(
                collective_id=which, has_side_effects=True, vmem_limit_bytes=VMEM_LIMIT),
        )

    most = live_count[0]
    if lax.axis_size("groups") > 1:
        most = lax.pmax(most, "groups")
    which = sum((most > n).astype(jnp.int32) for n in sizes[:-1])
    product = lax.switch(which, [call(n, i) for i, n in enumerate(sizes)], owner_map, tokens, stored)
    keep = lax.broadcasted_iota(jnp.int32, (rows, 1), 0) < live_count[0]
    return jnp.where(keep, product, jnp.bfloat16(0.0))


def solution(mesh):
    placed = (P(("tensor", "sub"), None), P(("groups", "tensor"), None), P(), P("groups"))
    return jax.shard_map(
        on_device,
        mesh=mesh,
        in_specs=placed,
        out_specs=P("groups", ("tensor", "sub")),
        check_vma=False,
    )
```

```python
import functools

import jax
import jax.numpy as jnp
from jax import lax
from jax.experimental import pallas as pl
from jax.experimental.pallas import tpu as pltpu
from jax.sharding import PartitionSpec as P

MESH = pl.DeviceIdType.MESH
VMEM_LIMIT = 67043328


def portable(stored, tokens, owner_map, live_count):
    row_count = stored.shape[0]
    block_count = owner_map.shape[0]
    width = stored.shape[1] // block_count
    devices = lax.axis_size(("tensor", "sub"))
    per_dev = block_count // devices
    ordered = jnp.take(stored.reshape(row_count, block_count, width), owner_map, axis=1)
    gathered = lax.all_gather(tokens, "tensor", axis=0, tiled=True)
    sectioned = ordered.reshape(row_count, devices, per_dev, width)
    piece = lax.all_to_all(sectioned, ("tensor", "sub"), split_axis=1, concat_axis=0, tiled=True)
    weights = piece.reshape(piece.shape[0], piece.shape[2], piece.shape[3])
    result = jnp.einsum("td,dkc->tkc", gathered, weights, preferred_element_type=jnp.float32)
    product = result.reshape(result.shape[0], per_dev * width)
    row_ids = lax.broadcasted_iota(jnp.int32, (product.shape[0], 1), 0)
    keep = row_ids < live_count[0]
    return jnp.where(keep, product, jnp.float32(0.0)).astype(jnp.bfloat16)


def kernel(T, own_rows, block, parts, map_ref, tok_ref, w_hbm, out_ref, w, tok, *refs):
    t = lax.axis_index("tensor")
    s = lax.axis_index("sub")
    depth = w.shape[1]
    other = 1 - s
    n = len(parts)
    bufs = [refs[7 * i:7 * i + 7] for i in range(n)]
    w_sem, ts, tr, ss, sr, cs, cr = refs[7 * n:]
    rows = bufs[0][2].shape[1]
    bits = [lax.rem(t // 2 ** k, 2) for k in range(4)]
    far = [t + 2 ** k * (1 - 2 * bits[k]) for k in range(4)]
    early = [i for i in range(n) if parts[i][1][0] == 2]
    per_dev = sum(count for count, _ in parts)
    starts = [sum(count for count, _ in parts[:i]) for i in range(n)]

    def load_block(b, carry):
        at = pl.multiple_of(b * block, block)
        pltpu.make_async_copy(w_hbm.at[:, pl.ds(at, block)], w.at[b], w_sem).start()
        return carry

    lax.fori_loop(0, w.shape[0], load_block, 0)

    barrier = pltpu.get_barrier_semaphore()
    for r in range(1, T):
        pl.semaphore_signal(barrier, inc=1, device_id={"tensor": lax.rem(t + r, T), "sub": s}, device_id_type=MESH)
    pl.semaphore_signal(barrier, inc=1, device_id={"tensor": t, "sub": other}, device_id_type=MESH)
    pl.semaphore_wait(barrier, T)

    def token_copy(r):
        to = lax.rem(t + r, T)
        return pltpu.make_async_remote_copy(
            src_ref=tok_ref.at[:, pl.ds(pl.multiple_of(to * 2 * depth, 2 * depth), 2 * depth)],
            dst_ref=tok.at[pl.ds(pl.multiple_of(t * own_rows, own_rows), own_rows), :],
            send_sem=ts.at[r], recv_sem=tr.at[r],
            device_id={"tensor": to, "sub": s}, device_id_type=MESH)

    for r in range(1, T):
        token_copy(r).start()
    tok[pl.ds(pl.multiple_of(t * own_rows, own_rows), own_rows), :] = (
        tok_ref[:, pl.ds(pl.multiple_of(t * 2 * depth, 2 * depth), 2 * depth)])

    def sub_copy(q, j, i):
        stage, wr = bufs[i][:2]
        return pltpu.make_async_remote_copy(
            src_ref=stage.at[j], dst_ref=wr.at[2 * q + j],
            send_sem=ss.at[2 * i + j], recv_sem=sr.at[16 * i + 2 * q + j],
            device_id={"tensor": t, "sub": other}, device_id_type=MESH)

    def halving(i, level, slot, at):
        place = 15 * i + (0, 8, 12, 14)[level] + at
        return pltpu.make_async_remote_copy(
            src_ref=bufs[i][2].at[slot], dst_ref=bufs[i][3 + level].at[at],
            send_sem=cs.at[place], recv_sem=cr.at[place],
            device_id={"tensor": far[parts[i][1][level]], "sub": s}, device_id_type=MESH)

    def first(g, j, i):
        return halving(i, 0, 4 * g + j, 2 * g + j)

    def second(g, i):
        return halving(i, 1, 4 * g + 2, g)

    def third(g, i):
        return halving(i, 2, 4 * g + 3, g)

    def fourth(i):
        return halving(i, 3, 11, 0)

    def add(i, level, slot, at):
        bufs[i][2][slot] += bufs[i][3 + level][at]

    def first_block(q, j, i, sub):
        g = q // 2
        flips = (1 - lax.rem(q, 2), 1 - j, 1 - g // 2, 1 - lax.rem(g, 2))
        to = 0
        for k, flip in zip(parts[i][1], flips):
            to += lax.rem(bits[k] + flip, 2) * 2 ** k
        return (2 * to + sub) * per_dev + starts[i]

    def columns(base, m):
        return w[map_ref[base + m]]

    def fill(q, j, i):
        base = first_block(q, j, i, other)
        for m in range(parts[i][0]):
            bufs[i][0][j, :, m * block:(m + 1) * block] = columns(base, m)
        sub_copy(q, j, i).start()

    pltpu.make_async_copy(w, w, w_sem).wait()
    for j in range(2):
        for i in range(n):
            fill(0, j, i)
    for r in range(1, T):
        token_copy(r).wait()

    def compute(q, carry):
        kept, g = lax.rem(q, 2), q // 2
        mine = tok[0:rows, pl.ds(pl.multiple_of(s * depth, depth), depth)]
        theirs = tok[0:rows, pl.ds(pl.multiple_of(other * depth, depth), depth)]
        for j in range(2):
            for i in range(n):
                base = first_block(q, j, i, s)
                own = jnp.concatenate([columns(base, m) for m in range(parts[i][0])], axis=1)
                total = jnp.dot(mine, own, preferred_element_type=jnp.float32)
                sub_copy(q, j, i).wait()
                total += jnp.dot(theirs, bufs[i][1][2 * q + j], preferred_element_type=jnp.float32)
                bufs[i][2][4 * g + 2 * kept + j] = total

                @pl.when((q == 0) if i not in early else (kept == 0))
                def _():
                    first(g, j, i).start()

                @pl.when(q < 7)
                def _():
                    fill(q + 1, j, i)
        return carry

    def finish(g):
        for i in range(n):
            second(g, i).wait_recv()
            add(i, 1, 4 * g + 3, g)

    def step(at, carry):
        g = at - 2

        @pl.when(g >= 0)
        def _():
            for i in range(n):
                first(g, 0, i).wait_recv()
                add(i, 0, 4 * g + 2, 2 * g)
                second(g, i).start()

            @pl.when(g < 3)
            def _():
                for j in range(2):
                    for i in range(n):
                        if i not in early:
                            first(g + 1, j, i).start()

            for i in range(n):
                first(g, 1, i).wait_recv()
                add(i, 0, 4 * g + 3, 2 * g + 1)

        lax.fori_loop(jnp.maximum(2 * g + 3, 0), jnp.minimum(2 * g + 5, 8), compute, 0)

        @pl.when(g >= 1)
        def _():
            finish(g - 1)

            @pl.when(g < 3)
            def _():
                for i in range(n):
                    third(g - 1, i).start()

            @pl.when(g == 3)
            def _():
                for i in range(n):
                    third(0, i).wait_recv()
                    add(i, 2, 11, 0)
                    fourth(i).start()
        return carry

    lax.fori_loop(0, 6, step, 0)
    for i in range(n):
        total = bufs[i][2][15]
        third(1, i).wait_recv()
        total += bufs[i][5][1]
        second(3, i).wait_recv()
        total += bufs[i][4][3]
        fourth(i).wait_recv()
        total += bufs[i][6][0]
        out_ref[0:rows, starts[i] * block:(starts[i] + parts[i][0]) * block] = total.astype(out_ref.dtype)
    for i in range(n):
        for g in range(4):
            for j in range(2):
                first(g, j, i).wait_send()
            second(g, i).wait_send()
        for g in range(2):
            third(g, i).wait_send()
        fourth(i).wait_send()


def split(per_dev):
    last = per_dev // 4
    rest = per_dev - last
    return (((rest + 1) // 2, (0, 1, 2, 3)), (rest // 2, (1, 0, 2, 3)), (last, (2, 3, 0, 1)))


def plan(depth, n_blocks, own_rows, block, T, parts, live):
    sems = pltpu.SemaphoreType.DMA
    f32, bf16 = jnp.float32, jnp.bfloat16
    n = len(parts)
    shapes = [pltpu.VMEM((n_blocks, depth, block), bf16), pltpu.VMEM((own_rows * T, 2 * depth), bf16)]
    for count, _ in parts:
        wide = count * block
        shapes += [pltpu.VMEM((2, depth, wide), bf16), pltpu.VMEM((16, depth, wide), bf16)]
        shapes += [pltpu.VMEM((k, live, wide), f32) for k in (16, 8, 4, 2, 1)]
    return shapes + [sems(()), sems((T,)), sems((T,)), sems((2 * n,)), sems((16 * n,)), sems((15 * n,)), sems((15 * n,))]


def fits(depth, ff, own_rows, T, subs, n_blocks):
    if T.bit_length() != 5 or T & (T - 1) or subs != 2 or n_blocks % (8 * T):
        return False
    rows, wide = own_rows * T, ff // (2 * T)
    used = 2 * (depth * ff + rows * 2 * depth + 18 * depth * wide) + 4 * 31 * rows * wide
    return used + (4 << 20) < VMEM_LIMIT


def on_device(stored, tokens, owner_map, live_count):
    depth, ff = stored.shape
    own_rows = tokens.shape[0]
    n_blocks = owner_map.shape[0]
    block = ff // n_blocks
    T, subs = lax.axis_size("tensor"), lax.axis_size("sub")
    if not fits(depth, ff, own_rows, T, subs, n_blocks):
        return portable(stored, tokens, owner_map, live_count)
    rows = own_rows * T
    parts = split(n_blocks // (2 * T))
    unit = max(rows // 16, 16)
    sizes = [n for n in range(rows - 8 * unit, rows, unit) if n > 0] + [rows]

    def call(n, which):
        return pl.pallas_call(
            functools.partial(kernel, T, own_rows, block, parts),
            out_shape=jax.ShapeDtypeStruct((rows, ff // (2 * T)), jnp.bfloat16),
            in_specs=[pl.BlockSpec(memory_space=pltpu.SMEM), pl.BlockSpec(memory_space=pltpu.VMEM),
                      pl.BlockSpec(memory_space=pl.ANY)],
            out_specs=pl.BlockSpec(memory_space=pltpu.VMEM),
            scratch_shapes=plan(depth, n_blocks, own_rows, block, T, parts, n),
            compiler_params=pltpu.CompilerParams(
                collective_id=which, has_side_effects=True, vmem_limit_bytes=VMEM_LIMIT),
        )

    most = live_count[0]
    if lax.axis_size("groups") > 1:
        most = lax.pmax(most, "groups")
    which = sum((most > n).astype(jnp.int32) for n in sizes[:-1])
    product = lax.switch(which, [call(n, i) for i, n in enumerate(sizes)], owner_map, tokens, stored)
    keep = lax.broadcasted_iota(jnp.int32, (rows, 1), 0) < live_count[0]
    return jnp.where(keep, product, jnp.bfloat16(0.0))


def solution(mesh):
    placed = (P(("tensor", "sub"), None), P(("groups", "tensor"), None), P(), P("groups"))
    return jax.shard_map(
        on_device,
        mesh=mesh,
        in_specs=placed,
        out_specs=P("groups", ("tensor", "sub")),
        check_vma=False,
    )
```
